32 devices in a mesh: ctx: 4 (over x, core), exp: 8 (over z, y).
Axes of the slice: x: 2, y: 2, z: 4, core: 2. Of those that a mesh axis runs over, the one named last changes fastest.
Arguments:
- queries: bfloat16 [8, 512, 1536], P('exp', 'ctx'), may hold values from -2.5 to 2.5
- key_states: bfloat16 [8, 512, 1536], P('exp', 'ctx'), may hold values from -2.5 to 2.5
- value_states: bfloat16 [8, 512, 1536], P('exp', 'ctx'), may hold values from -6 to 6
- attended: bfloat16 [8, 512, 1536], P('exp', 'ctx'), may hold values from -6 to 6
- output_grad: bfloat16 [8, 512, 1536], P('exp', 'ctx'), may hold values from -6 to 6
- expert_ids: int32 [8, 512, 2], P('exp', 'ctx'), may hold values from 0 to 7, all different within a row; in each aligned block of 128 rows (0 to 127, 128 to 255, ..., all dimensions but the last counted through in order) at most 48 rows name the same one
- gate_weights: float32 [8, 512, 2], P('exp', 'ctx'), may hold values from 0.2 to 1
- w_in: bfloat16 [8, 1536, 768], P('exp'), may hold values from -0.15625 to 0.15625
- w_out: bfloat16 [8, 768, 1536], P('exp'), may hold values from -0.21875 to 0.21875
Outputs:
- query_grad: bfloat16 [8, 512, 1536], P('exp', 'ctx')
- key_grad: bfloat16 [8, 512, 1536], P('exp', 'ctx')
- value_grad: bfloat16 [8, 512, 1536], P('exp', 'ctx')
- w_in_grad: bfloat16 [8, 1536, 768], P('exp', 'ctx')
- w_out_grad: bfloat16 [8, 768, 1536], P('exp', 'ctx')
The draws below stay inside these ranges and needn't reach their ends.
Inputs may be any that keep to these rules, and one draw needn't show every extreme that they name: `expert_ids`: in each aligned block of 128 frames (the frames of one device) no expert is named by more than 48 frames, a bound that some block reaches; the two experts of a frame differ.
All inputs are finite; a program needn't handle non-finite values.
Results may differ from the reference program's by a relative error of at most 0.02.
Values may be sent and summed in bfloat16 or wider, within the bound.
No kernel may reach another device: no remote copies, remote signals or barrier semaphores. Data moves between devices by JAX's collectives and lax.ppermute only.
A program may use at most 128 MiB of HBM per device.

```python
import math
import jax
import jax.numpy as jnp
import numpy as np
from jax import lax

HEADS = 12
HEAD_DIM = 128
D = 1536
FF = 768
TOK = 128
EXPERTS = 8
BATCH = 8
LEN = 512
CAP = 48
N_CTX = 4


def shard_levels(rng, dims, pieces, smallest, high):
    level, own = 1.0, jax.random.fold_in(rng, 6)
    for position, blocks in pieces:
        steps = jnp.exp(jax.random.uniform(jax.random.fold_in(own, position), (blocks,), jnp.float32, smallest / len(pieces), high / len(pieces)))
        level = level * jnp.repeat(steps, dims[position] // blocks).reshape([-1 if axis == position else 1 for axis in range(len(dims))])
    return level


def shared_out(rng, own, number, rows, number_of, top, reach, skew):
    order = jax.random.permutation(rng, number_of)
    heavy_load, ordinary = shares(number_of, rows * top, reach, skew, True), shares(number_of, rows * top, reach, skew, False)
    places = jnp.arange(number_of)

    def named(tallies, turn):
        used = int((tallies > 0).sum())
        fixed = max(1, used // 4)
        shifted = fixed + (places - fixed + turn * (used - fixed)) % max(1, number_of - fixed)
        return jnp.zeros((number_of,), jnp.int32).at[order[jnp.where(places < fixed, places, shifted)]].set(jnp.asarray(tallies, jnp.int32))

    tallies = jnp.where(number % 4 == 0, named(heavy_load, number // 4), named(ordinary, number - number // 4 - 1))
    mixed = jax.random.permutation(jax.random.fold_in(own, 3), number_of)
    donor, receiver = mixed[0:number_of // 2 * 2:2], mixed[1:number_of // 2 * 2:2]
    slack = jnp.minimum(tallies[donor] - 1, reach - tallies[receiver]) // 2
    slack = jnp.where((donor == order[0]) | (receiver == order[0]) | (tallies[receiver] == 0), 0, jnp.maximum(slack, 0))
    shifted = jax.random.randint(jax.random.fold_in(own, 4), (number_of // 2,), 0, 1 << 20) % (slack + 1)
    tallies = tallies.at[donor].add(-shifted).at[receiver].add(shifted)
    items = jnp.searchsorted(jnp.cumsum(tallies), jnp.arange(rows * top), side="right").astype(jnp.int32)
    table = items.reshape(top, rows).T
    table = table[jax.random.permutation(jax.random.fold_in(own, 1), rows)]
    turn = jax.random.randint(jax.random.fold_in(own, 2), (rows, 1), 0, top)
    return jnp.take_along_axis(table, (jnp.arange(top)[None, :] + turn) % top, axis=1)


def shares(count, total, reach, lean, full):
    weights = [(1 << 20) // math.isqrt(standing ** lean) + 1 for standing in range(1, count + 1)]
    largest = reach if full else min(reach, max(-(-total // count), total * weights[0] // sum(weights)))
    least = 1 if total - largest >= count - 1 else 0
    given, spare = [largest] + [least] * (count - 1), total - largest - least * (count - 1)
    while spare > 0:
        free = [i for i in range(1, count) if given[i] < largest] or [i for i in range(1, count) if given[i] < reach]
        mass, budget = sum([weights[i] for i in free]), spare
        for i in free:
            addition = min(reach - given[i], max(1, budget * weights[i] // mass), spare)
            given[i] = given[i] + addition
            spare = spare - addition
    return np.array(given)


def bell_draw(key, extent, scale, most, cuts=(), held_as=jnp.bfloat16):
    array = jax.random.normal(key, extent, jnp.float32) * scale
    if len(cuts) > 0:
        array = shard_levels(key, extent, cuts, -0.22, 0.18) * array
    return jnp.clip(array, min=-most, max=most).astype(held_as)


def setup_inputs(seed: int = 0) -> dict:
    key_list = jax.random.split(jax.random.key(seed), 10)
    queries = bell_draw(key_list[0], (BATCH, LEN, D), 1.0, 2.5, ((0, 8), (1, 4)))
    key_states = bell_draw(key_list[1], (BATCH, LEN, D), 1.0, 2.5, ((0, 8), (1, 4)))
    value_states = bell_draw(key_list[2], (BATCH, LEN, D), 1.0, 6.0, ((0, 8), (1, 4)))
    attended = bell_draw(key_list[3], (BATCH, LEN, D), 1.0, 6.0, ((0, 8), (1, 4)))
    output_grad = bell_draw(key_list[4], (BATCH, LEN, D), 1.0, 6.0, ((0, 8), (1, 4)))
    expert_ids_keys = jax.random.split(jax.random.fold_in(key_list[5], 1), BATCH * LEN // TOK)
    expert_ids_turns = jax.random.permutation(jax.random.fold_in(key_list[5], 3), BATCH * LEN // TOK)
    expert_ids = jax.vmap(lambda own, number: shared_out(jax.random.fold_in(key_list[5], 2), own, number, TOK, EXPERTS, 2, CAP, 2))(expert_ids_keys, expert_ids_turns).reshape((BATCH, LEN, 2))
    gate_weights = jnp.clip(0.2 + 0.8 * jax.random.uniform(key_list[6], (BATCH, LEN, 2), jnp.float32) ** shard_levels(key_list[6], (BATCH, LEN, 2), ((0, 8), (1, 4)), -0.2, 0.2), 0.2, 1.0)
    w_in = bell_draw(key_list[7], (EXPERTS, D, FF), D ** -0.5, 0.15625, ((0, 8),))
    w_out = bell_draw(key_list[8], (EXPERTS, FF, D), FF ** -0.5, 0.21875, ((0, 8),))
    return {"queries": queries, "key_states": key_states, "value_states": value_states, "attended": attended, "output_grad": output_grad, "expert_ids": expert_ids, "gate_weights": gate_weights, "w_in": w_in, "w_out": w_out}


def rounded(x):
    return lax.optimization_barrier(x.astype(jnp.bfloat16)).astype(jnp.float32)


def expert_part(attended, output_grad, expert_ids, gate_weights, w_in, w_out):
    flat_rows = attended.reshape(-1, D)
    flat_grad = output_grad.reshape(-1, D)
    nrows = flat_rows.shape[0]
    nblocks = nrows // TOK
    route = expert_ids.reshape(nblocks, TOK * 2).astype(jnp.int32)
    onehot = (route[:, :, None] == jnp.arange(EXPERTS, dtype=jnp.int32)[None, None, :]).astype(jnp.int32)
    slot = jnp.sum((jnp.cumsum(onehot, axis=1) - 1) * onehot, axis=2).astype(jnp.int32)
    pair_expert = route.reshape(-1)
    pair_slot = slot.reshape(-1)
    pair_index = jnp.arange(nblocks * TOK * 2, dtype=jnp.int32)
    pair_block = pair_index // (TOK * 2)
    pair_row = pair_index // 2
    rows_buf = jnp.zeros((EXPERTS, nblocks, CAP, D), jnp.bfloat16)
    rows_buf = rows_buf.at[pair_expert, pair_block, pair_slot].set(flat_rows[pair_row])
    row_grad = (gate_weights.reshape(-1)[:, None] * flat_grad[pair_row].astype(jnp.float32)).astype(jnp.bfloat16)
    grad_buf = jnp.zeros((EXPERTS, nblocks, CAP, D), jnp.bfloat16)
    grad_buf = grad_buf.at[pair_expert, pair_block, pair_slot].set(row_grad)

    def one_expert(item):
        rows, grads, w_first, w_second = item
        upper = jnp.einsum("ncd,df->ncf", rows.astype(jnp.float32), w_first.astype(jnp.float32))
        sig = jax.nn.sigmoid(upper)
        act = (upper * sig).astype(jnp.bfloat16)
        act_grad = jnp.einsum("ncd,fd->ncf", grads.astype(jnp.float32), w_second.astype(jnp.float32))
        up_grad = (act_grad * sig * (1.0 + upper * (1.0 - sig))).astype(jnp.bfloat16)
        row_back = jnp.einsum("ncf,df->ncd", up_grad.astype(jnp.float32), w_first.astype(jnp.float32)).astype(jnp.bfloat16)
        rows_c = rows.reshape(BATCH, N_CTX, CAP, D).astype(jnp.float32)
        grads_c = grads.reshape(BATCH, N_CTX, CAP, D).astype(jnp.float32)
        upg_c = up_grad.reshape(BATCH, N_CTX, CAP, FF).astype(jnp.float32)
        act_c = act.reshape(BATCH, N_CTX, CAP, FF).astype(jnp.float32)
        first_grad = jnp.sum(rounded(jnp.einsum("bcsd,bcsf->cdf", rows_c, upg_c)), axis=0).astype(jnp.bfloat16)
        second_grad = jnp.sum(rounded(jnp.einsum("bcsf,bcsd->cfd", act_c, grads_c)), axis=0).astype(jnp.bfloat16)
        return row_back, first_grad, second_grad

    back_buf, w_in_grad, w_out_grad = lax.map(one_expert, (rows_buf, grad_buf, w_in, w_out))
    back = back_buf[pair_expert, pair_block, pair_slot].astype(jnp.float32).reshape(nrows, 2, D)
    attn_grad = (flat_grad.astype(jnp.float32) + back[:, 0] + back[:, 1]).astype(jnp.bfloat16)
    return attn_grad.reshape(BATCH, LEN, D), w_in_grad, w_out_grad


def attention_stream(item):
    queries, key_states, value_states, attended, attn_grad = item
    scale = HEAD_DIM ** -0.5
    q_all = queries.astype(jnp.float32).reshape(N_CTX, TOK, HEADS, HEAD_DIM)
    k_all = key_states.astype(jnp.float32).reshape(LEN, HEADS, HEAD_DIM)
    v_all = value_states.astype(jnp.float32).reshape(LEN, HEADS, HEAD_DIM)
    k_blocks = k_all.reshape(N_CTX, TOK, HEADS, HEAD_DIM)
    g_all = attn_grad.astype(jnp.float32).reshape(N_CTX, TOK, HEADS, HEAD_DIM)
    delta_all = jnp.sum(g_all * attended.astype(jnp.float32).reshape(N_CTX, TOK, HEADS, HEAD_DIM), axis=3)

    def step(carry, blk):
        key_acc, value_acc = carry
        q_blk, g_blk, d_blk = blk
        scores = jnp.einsum("qhd,khd->hqk", q_blk, k_all) * scale
        norm_log = jnp.log(jnp.sum(jnp.exp(scores), axis=2))
        probs = jnp.exp(scores - norm_log[:, :, None])
        probs_b = probs.astype(jnp.bfloat16).astype(jnp.float32)
        prob_grad = jnp.einsum("qhd,khd->hqk", g_blk, v_all)
        score_grad = (probs * (prob_grad - d_blk.T[:, :, None])).astype(jnp.bfloat16).astype(jnp.float32)
        split = score_grad.reshape(HEADS, TOK, N_CTX, TOK)
        q_part = jnp.einsum("hqck,ckhd->cqhd", split, k_blocks) * scale
        q_grad = jnp.sum(rounded(q_part), axis=0).astype(jnp.bfloat16)
        key_acc = key_acc + rounded(jnp.einsum("hqk,qhd->khd", score_grad, q_blk) * scale)
        value_acc = value_acc + rounded(jnp.einsum("hqk,qhd->khd", probs_b, g_blk))
        return (key_acc, value_acc), q_grad

    zero = jnp.zeros((LEN, HEADS, HEAD_DIM), jnp.float32)
    (key_acc, value_acc), q_grads = lax.scan(step, (zero, zero), (q_all, g_all, delta_all))
    return (q_grads.reshape(LEN, D), key_acc.reshape(LEN, D).astype(jnp.bfloat16),
            value_acc.reshape(LEN, D).astype(jnp.bfloat16))


def reference(queries, key_states, value_states, attended, output_grad, expert_ids, gate_weights, w_in, w_out):
    attn_grad, w_in_grad, w_out_grad = expert_part(attended, output_grad, expert_ids, gate_weights, w_in, w_out)
    query_grad, key_grad, value_grad = lax.map(attention_stream, (queries, key_states, value_states, attended, attn_grad))
    return query_grad, key_grad, value_grad, w_in_grad, w_out_grad
```

```python
import jax
import jax.numpy as jnp
from jax import lax
from jax.experimental import pallas as pl
from jax.experimental.pallas import tpu as pltpu
from jax.sharding import PartitionSpec as P

HEAD_DIM = 128
EXP_DEV = 1


def rounded(x):
    return lax.optimization_barrier(x.astype(jnp.bfloat16)).astype(jnp.float32)


def general(
    queries, key_states, value_states, attended, output_grad, expert_ids, gate_weights, w_in, w_out
):
    tok = queries.shape[1]
    width = queries.shape[2]
    heads = width // HEAD_DIM
    nexp = lax.axis_size("exp")
    nctx = lax.axis_size("ctx")
    experts = EXP_DEV * nexp
    capacity = 3 * tok // experts
    attn_rows = attended[0]
    grad_rows = output_grad[0]
    route = expert_ids[0].reshape(-1)
    gates = gate_weights[0].reshape(-1)
    onehot = (route[:, None] == jnp.arange(experts, dtype=jnp.int32)[None, :]).astype(jnp.int32)
    slots = jnp.sum((jnp.cumsum(onehot, axis=0) - 1) * onehot, axis=1)
    target = route * capacity + slots
    placed = target[None, :] == jnp.arange(experts * capacity, dtype=jnp.int32)[:, None]
    picker = (
        placed.reshape(experts * capacity, tok, 2)
        .astype(jnp.float32)
        .sum(axis=2)
        .astype(jnp.bfloat16)
    )
    slot_gate = jnp.sum(jnp.where(placed, gates[None, :], 0.0), axis=1)
    sent_rows = jnp.dot(picker, attn_rows, preferred_element_type=jnp.float32).astype(jnp.bfloat16)
    sent_grads = (
        jnp.dot(picker, grad_rows, preferred_element_type=jnp.float32) * slot_gate[:, None]
    ).astype(jnp.bfloat16)
    shape = (nexp, EXP_DEV * capacity, width)
    got_rows, got_grads = (
        lax.all_to_all(sent_rows.reshape(shape), "exp", split_axis=0, concat_axis=0, tiled=True),
        lax.all_to_all(sent_grads.reshape(shape), "exp", split_axis=0, concat_axis=0, tiled=True),
    )

    def by_expert(values):
        return (
            values.reshape(nexp, EXP_DEV, capacity, -1)
            .transpose(1, 0, 2, 3)
            .reshape(EXP_DEV, nexp * capacity, -1)
        )

    rows_in = by_expert(got_rows)
    grads_in = by_expert(got_grads)
    upper = jnp.einsum("erd,edf->erf", rows_in, w_in, preferred_element_type=jnp.float32)
    sig = jax.nn.sigmoid(upper)
    act = (upper * sig).astype(jnp.bfloat16)
    act_grad = jnp.einsum("erd,efd->erf", grads_in, w_out, preferred_element_type=jnp.float32)
    up_grad = (act_grad * sig * (1.0 + upper * (1.0 - sig))).astype(jnp.bfloat16)
    row_back = jnp.einsum("erf,edf->erd", up_grad, w_in, preferred_element_type=jnp.float32).astype(
        jnp.bfloat16
    )
    first_term = jnp.einsum("erd,erf->edf", rows_in, up_grad, preferred_element_type=jnp.float32)
    second_term = jnp.einsum("erf,erd->efd", act, grads_in, preferred_element_type=jnp.float32)
    back_send = (
        row_back.reshape(EXP_DEV, nexp, capacity, width).transpose(1, 0, 2, 3).reshape(shape)
    )
    returned = lax.all_to_all(back_send, "exp", split_axis=0, concat_axis=0, tiled=True)
    back_sum = jnp.dot(
        picker.T, returned.reshape(experts * capacity, width), preferred_element_type=jnp.float32
    )
    attn_grad = (grad_rows.astype(jnp.float32) + back_sum).astype(jnp.bfloat16)
    first_sum, second_sum = (
        lax.psum_scatter(
            first_term.astype(jnp.bfloat16), "ctx", scatter_dimension=1, tiled=True
        ).astype(jnp.float32),
        lax.psum_scatter(
            second_term.astype(jnp.bfloat16), "ctx", scatter_dimension=1, tiled=True
        ).astype(jnp.float32),
    )
    w_in_grad = first_sum.astype(jnp.bfloat16)
    w_out_grad = second_sum.astype(jnp.bfloat16)
    scale = HEAD_DIM ** (-0.5)
    group = min(max(1, 512 // tok), nctx)
    blocks = nctx // group
    key_heads = key_states[0].reshape(tok, heads, HEAD_DIM)
    value_heads = value_states[0].reshape(tok, heads, HEAD_DIM)
    delta = jnp.sum(
        (attn_grad.astype(jnp.float32) * attn_rows.astype(jnp.float32)).reshape(
            tok, heads, HEAD_DIM
        ),
        axis=2,
    )
    query_all, grad_all = (
        lax.all_gather(queries[0], "ctx", axis=0, tiled=True),
        lax.all_gather(attn_grad, "ctx", axis=0, tiled=True),
    )
    span = group * tok
    query_blocks = query_all.reshape(blocks, span, heads, HEAD_DIM)
    grad_blocks = grad_all.reshape(blocks, span, heads, HEAD_DIM)

    def norm_part(carry, query_blk):
        scores = (
            jnp.einsum("qhd,khd->hqk", query_blk, key_heads, preferred_element_type=jnp.float32)
            * scale
        )
        return (carry, jnp.sum(jnp.exp(scores), axis=2).T)

    _, partial_sums = lax.scan(norm_part, jnp.zeros((), jnp.float32), query_blocks)
    own_delta = jnp.zeros((nctx * tok, heads), jnp.float32)
    own_delta = lax.dynamic_update_slice(own_delta, delta, (lax.axis_index("ctx") * tok, 0))
    totals, delta_all = (
        lax.psum(partial_sums.reshape(nctx * tok, heads).astype(jnp.bfloat16), "ctx").astype(
            jnp.float32
        ),
        lax.psum(own_delta.astype(jnp.bfloat16), "ctx").astype(jnp.float32),
    )
    norm_blocks = jnp.log(totals).reshape(blocks, span, heads)
    delta_blocks = delta_all.reshape(blocks, span, heads)

    def grad_step(carry, blk):
        key_acc, value_acc = carry
        query_blk, grad_blk, norm_blk, delta_blk = blk
        scores = (
            jnp.einsum("qhd,khd->hqk", query_blk, key_heads, preferred_element_type=jnp.float32)
            * scale
        )
        probs = jnp.exp(scores - norm_blk.T[:, :, None])
        probs_b = probs.astype(jnp.bfloat16)
        prob_grad = jnp.einsum(
            "qhd,khd->hqk", grad_blk, value_heads, preferred_element_type=jnp.float32
        )
        score_grad = (probs * (prob_grad - delta_blk.T[:, :, None])).astype(jnp.bfloat16)
        query_term = (
            jnp.einsum("hqk,khd->qhd", score_grad, key_heads, preferred_element_type=jnp.float32)
            * scale
        )
        split_grad = score_grad.reshape(heads, group, tok, tok)
        split_probs = probs_b.reshape(heads, group, tok, tok)
        split_query = query_blk.reshape(group, tok, heads, HEAD_DIM)
        split_out = grad_blk.reshape(group, tok, heads, HEAD_DIM)
        key_part = (
            jnp.einsum(
                "hgqk,gqhd->gkhd", split_grad, split_query, preferred_element_type=jnp.float32
            )
            * scale
        )
        value_part = jnp.einsum(
            "hgqk,gqhd->gkhd", split_probs, split_out, preferred_element_type=jnp.float32
        )
        key_acc = key_acc + jnp.sum(rounded(key_part), axis=0)
        value_acc = value_acc + jnp.sum(rounded(value_part), axis=0)
        return ((key_acc, value_acc), query_term)

    zero = jnp.zeros((tok, heads, HEAD_DIM), jnp.float32)
    (key_acc, value_acc), query_terms = lax.scan(
        grad_step, (zero, zero), (query_blocks, grad_blocks, norm_blocks, delta_blocks)
    )
    query_sum = lax.psum_scatter(
        query_terms.reshape(nctx * tok, width).astype(jnp.bfloat16),
        "ctx",
        scatter_dimension=0,
        tiled=True,
    )
    key_grad = key_acc.reshape(tok, width).astype(jnp.bfloat16)
    value_grad = value_acc.reshape(tok, width).astype(jnp.bfloat16)
    return (query_sum[None], key_grad[None], value_grad[None], w_in_grad, w_out_grad)


F32, BF16 = jnp.float32, jnp.bfloat16
NT = (((1,), (1,)), ((), ()))
TN = (((0,), (0,)), ((), ()))
WIDE = 512


def vmem_specs(count):
    return [pl.BlockSpec(memory_space=pltpu.VMEM)] * count


def pick_rows(ids, gates, rows, experts, capacity):
    tok, width = rows.shape

    def kernel(ids_ref, gates_ref, rows_ref, out_ref, pick_ref, gate_ref):
        first, second = ids_ref[0:1, :], ids_ref[1:2, :]
        expert = lax.broadcasted_iota(jnp.int32, (experts, tok), 0)
        is_first, is_second = first == expert, second == expert
        member = jnp.where(is_first | is_second, 1.0, 0.0)
        earlier = jnp.where(
            lax.broadcasted_iota(jnp.int32, (tok, tok), 0)
            < lax.broadcasted_iota(jnp.int32, (tok, tok), 1),
            1.0,
            0.0,
        )
        before = jnp.dot(member.astype(BF16), earlier.astype(BF16), preferred_element_type=F32)
        slot = jnp.where(member > 0, before, -1.0).astype(jnp.int32)
        gate = jnp.where(is_first, gates_ref[0:1, :], 0.0) + jnp.where(
            is_second, gates_ref[1:2, :], 0.0
        )
        place = lax.broadcasted_iota(jnp.int32, (capacity, tok), 0)
        for e in range(experts):
            chosen = jnp.where(slot[e : e + 1, :] == place, 1.0, 0.0)
            span = slice(e * capacity, (e + 1) * capacity)
            pick_ref[span, :] = chosen.astype(BF16)
            gate_ref[span, :] = jnp.sum(chosen * gate[e : e + 1, :], axis=1, keepdims=True)
        pick = pick_ref[...]
        for n in range(0, width, WIDE):
            part = jnp.dot(pick, rows_ref[:, n : n + WIDE], preferred_element_type=F32)
            out_ref[:, :, n : n + WIDE] = part.astype(BF16).reshape(experts, capacity, WIDE)

    return pl.pallas_call(
        kernel,
        out_shape=(
            jax.ShapeDtypeStruct((experts, capacity, width), BF16),
            jax.ShapeDtypeStruct((experts * capacity, tok), BF16),
            jax.ShapeDtypeStruct((experts * capacity, 1), F32),
        ),
        in_specs=vmem_specs(3),
        out_specs=tuple(vmem_specs(3)),
        name="pick_rows",
    )(ids, gates, rows)


def pick_grads(pick, gate, grads, experts, capacity):
    tok, width = grads.shape

    def kernel(pick_ref, gate_ref, grads_ref, out_ref):
        pick, gate = pick_ref[...], gate_ref[...]
        for n in range(0, width, WIDE):
            part = jnp.dot(pick, grads_ref[:, n : n + WIDE], preferred_element_type=F32) * gate
            out_ref[:, :, n : n + WIDE] = part.astype(BF16).reshape(experts, capacity, WIDE)

    return pl.pallas_call(
        kernel,
        out_shape=jax.ShapeDtypeStruct((experts, capacity, width), BF16),
        in_specs=vmem_specs(3),
        out_specs=pl.BlockSpec(memory_space=pltpu.VMEM),
        name="pick_grads",
    )(pick, gate, grads)


def add_back(pick, returned, grads):
    tok, width = grads.shape

    def kernel(pick_ref, back_ref, grads_ref, out_ref):
        back = back_ref[...].reshape(-1, width)
        total = lax.dot_general(pick_ref[...], back, TN, preferred_element_type=F32)
        out_ref[...] = (grads_ref[...].astype(F32) + total).astype(BF16)

    return pl.pallas_call(
        kernel,
        out_shape=jax.ShapeDtypeStruct((tok, width), BF16),
        in_specs=vmem_specs(3),
        out_specs=pl.BlockSpec(memory_space=pltpu.VMEM),
        name="add_back",
    )(pick, returned, grads)


def head_specs(count, tok, first=0):
    return [pl.BlockSpec((tok, HEAD_DIM), lambda h: (0, h + first))] * count


def probabilities(query_blocks, key_blocks):
    tok, width = query_blocks[0].shape
    heads, count = width // HEAD_DIM, len(query_blocks)
    total = count * tok
    scale = HEAD_DIM**-0.5

    def kernel(*refs):
        q = jnp.concatenate([r[...] for r in refs[:count]], axis=0)
        k = jnp.concatenate([r[...] for r in refs[count : 2 * count]], axis=0)
        by_query_ref, by_key_ref = refs[2 * count :]
        row = jnp.exp(
            lax.dot_general(q[:tok], k, NT, preferred_element_type=F32) * scale
        )
        by_query_ref[0] = (row / jnp.sum(row, axis=1, keepdims=True)).astype(BF16)
        col = jnp.exp(lax.dot_general(k[:tok], q, NT, preferred_element_type=F32) * scale)
        norm = jnp.sum(col, axis=0, keepdims=True)
        for b in range(1, count):
            other = lax.dot_general(
                k[b * tok : (b + 1) * tok], q, NT, preferred_element_type=F32
            )
            norm = norm + jnp.sum(jnp.exp(other * scale), axis=0, keepdims=True)
        by_key_ref[0] = (col / norm).astype(BF16)

    shape = jax.ShapeDtypeStruct((heads, tok, total), BF16)
    return pl.pallas_call(
        kernel,
        grid=(heads,),
        out_shape=(shape, shape),
        in_specs=head_specs(2 * count, tok),
        out_specs=(pl.BlockSpec((1, tok, total), lambda h: (h, 0, 0)),) * 2,
        name="probabilities",
    )(*query_blocks, *key_blocks)


def query_side(span, g, attended, probs, key_blocks, value_blocks, before):
    first, last = span
    tok, width = attended.shape
    count = len(key_blocks)
    scale = HEAD_DIM**-0.5
    carried = [] if before is None else [before]

    def kernel(*refs):
        g_ref, att_ref, probs_ref = refs[:3]
        k = jnp.concatenate([r[...] for r in refs[3 : 3 + count]], axis=0)
        v = jnp.concatenate([r[...] for r in refs[3 + count : 3 + 2 * count]], axis=0)
        out_ref = refs[-1]
        g = g_ref[...]
        both = jnp.concatenate(
            [g, (g.astype(F32) * att_ref[...].astype(F32)).astype(BF16)], axis=1
        )
        v = jnp.concatenate([v, jnp.full_like(v, -1.0)], axis=1)
        diff = lax.dot_general(both, v, NT, preferred_element_type=F32)
        score = (probs_ref[0].astype(F32) * diff).astype(BF16)
        out_ref[...] = (jnp.dot(score, k, preferred_element_type=F32) * scale).astype(BF16)

    return pl.pallas_call(
        kernel,
        grid=(last - first,),
        out_shape=jax.ShapeDtypeStruct((tok, width), BF16),
        in_specs=head_specs(1, tok)
        + head_specs(1, tok, first)
        + [pl.BlockSpec((1, tok, count * tok), lambda h: (h + first, 0, 0))]
        + head_specs(2 * count, tok, first)
        + [pl.BlockSpec(memory_space=pl.ANY)] * len(carried),
        out_specs=head_specs(1, tok, first)[0],
        input_output_aliases={3 + 2 * count: 0} if carried else {},
        name="query_side",
    )(g, attended, probs, *key_blocks, *value_blocks, *carried)


def key_side(span, g_blocks, attended_blocks, probs, query_blocks, values, before):
    first, last = span
    tok, width = values.shape
    count = len(g_blocks)
    scale = HEAD_DIM**-0.5
    carried = [] if before is None else list(before)

    def kernel(*refs):
        probs_ref, v_ref = refs[:2]
        g = jnp.concatenate([r[...] for r in refs[2 : 2 + count]], axis=0)
        att = jnp.concatenate([r[...] for r in refs[2 + count : 2 + 2 * count]], axis=0)
        q = jnp.concatenate([r[...] for r in refs[2 + 2 * count : 2 + 3 * count]], axis=0)
        key_ref, value_ref = refs[-2:]
        both = jnp.concatenate([g, (g.astype(F32) * att.astype(F32)).astype(BF16)], axis=1)
        v = v_ref[...]
        v = jnp.concatenate([v, jnp.full_like(v, -1.0)], axis=1)
        diff = lax.dot_general(v, both, NT, preferred_element_type=F32)
        probs = probs_ref[0]
        score = (probs.astype(F32) * diff).astype(BF16)
        key_ref[...] = (jnp.dot(score, q, preferred_element_type=F32) * scale).astype(BF16)
        value_ref[...] = jnp.dot(probs, g, preferred_element_type=F32).astype(BF16)

    shape = jax.ShapeDtypeStruct((tok, width), BF16)
    return pl.pallas_call(
        kernel,
        grid=(last - first,),
        out_shape=(shape, shape),
        in_specs=[pl.BlockSpec((1, tok, count * tok), lambda h: (h + first, 0, 0))]
        + head_specs(1, tok, first)
        + head_specs(count, tok)
        + head_specs(2 * count, tok, first)
        + [pl.BlockSpec(memory_space=pl.ANY)] * len(carried),
        out_specs=tuple(head_specs(2, tok, first)),
        input_output_aliases={2 + 3 * count: 0, 3 + 3 * count: 1} if carried else {},
        name="key_side",
    )(probs, values, *g_blocks, *attended_blocks, *query_blocks, *carried)


def swap(values, axis, bit):
    return lax.ppermute(values, axis, [(i, i ^ bit) for i in range(lax.axis_size(axis))])


def stream_blocks(own):
    across = swap(own, "ctx", 2)
    return own, swap(own, "ctx", 1), across, swap(across, "ctx", 1)


def share_rows(term):
    place = lax.axis_index("ctx")
    core, chip = place % 2, place // 2
    split = term.astype(BF16).reshape(2, 2, term.shape[0] // 4, term.shape[1])
    kept = lax.dynamic_index_in_dim(split, core, 1, keepdims=False)
    sent = lax.dynamic_index_in_dim(split, 1 - core, 1, keepdims=False)
    half = (kept.astype(F32) + swap(sent, "ctx", 1).astype(F32)).astype(BF16)
    kept = lax.dynamic_index_in_dim(half, chip, 0, keepdims=False)
    sent = lax.dynamic_index_in_dim(half, 1 - chip, 0, keepdims=False)
    return (kept.astype(F32) + swap(sent, "ctx", 2).astype(F32)).astype(BF16)


def exchange(values):
    return lax.all_to_all(values, "exp", split_axis=0, concat_axis=0, tiled=True)


def quick(
    queries, key_states, value_states, attended, output_grad, expert_ids, gate_weights, w_in, w_out
):
    tok, width = queries.shape[1:]
    heads = width // HEAD_DIM
    experts = lax.axis_size("exp")
    capacity = 3 * tok // experts
    w_first, w_second = w_in[0], w_out[0]
    ids, gates = expert_ids[0].T, gate_weights[0].T
    attn_rows, grad_rows = attended[0], output_grad[0]

    sent_rows, pick, slot_gate = pick_rows(ids, gates, attn_rows, experts, capacity)
    got_rows = exchange(sent_rows)
    sent_grads = pick_grads(pick, slot_gate, grad_rows, experts, capacity)
    got_grads = exchange(sent_grads)

    query_blocks = stream_blocks(queries[0])
    key_blocks = stream_blocks(key_states[0])
    value_blocks = stream_blocks(value_states[0])
    attended_blocks = stream_blocks(attn_rows)
    by_query, by_key = probabilities(query_blocks, key_blocks)

    rows_in = got_rows.reshape(-1, width)
    grads_in = got_grads.reshape(-1, width)
    upper = jnp.dot(rows_in, w_first, preferred_element_type=F32)
    sig = jax.nn.sigmoid(upper)
    act = (upper * sig).astype(BF16)
    act_grad = lax.dot_general(grads_in, w_second, NT, preferred_element_type=F32)
    up_grad = (act_grad * sig * (1.0 + upper * (1.0 - sig))).astype(BF16)

    spans = ((0, 2 * heads // 3), (2 * heads // 3, heads))
    query_grad = pair = None
    first_term = lax.dot_general(rows_in, up_grad, TN, preferred_element_type=F32)
    second_term = lax.dot_general(act, grads_in, TN, preferred_element_type=F32)
    w_out_grad = share_rows(second_term)
    w_in_grad = share_rows(first_term)
    for first, last in spans:
        cols = slice(first * HEAD_DIM, last * HEAD_DIM)
        row_back = lax.dot_general(
            up_grad, w_first[cols], NT, preferred_element_type=F32
        ).astype(BF16)
        returned = exchange(row_back.reshape(experts, capacity, -1))
        g = add_back(pick, returned, grad_rows[:, cols])
        g_blocks = stream_blocks(g)
        query_grad = query_side(
            (first, last), g, attn_rows, by_query, key_blocks, value_blocks, query_grad
        )
        pair = key_side(
            (first, last), g_blocks, attended_blocks, by_key, query_blocks, value_states[0], pair
        )
    key_grad, value_grad = pair
    return (query_grad[None], key_grad[None], value_grad[None], w_in_grad[None], w_out_grad[None])


def per_device(queries, *rest):
    tok, width = queries.shape[1:]
    capacity = 3 * tok // lax.axis_size("exp")
    fits = lax.axis_size("ctx") == 4 and tok % 128 == 0 and capacity % 16 == 0
    if fits and width % (3 * HEAD_DIM) == 0 and width % WIDE == 0:
        return quick(queries, *rest)
    return general(queries, *rest)


def solution(mesh):
    return jax.shard_map(
        per_device,
        mesh=mesh,
        in_specs=(
            P("exp", "ctx", None),
            P("exp", "ctx", None),
            P("exp", "ctx", None),
            P("exp", "ctx", None),
            P("exp", "ctx", None),
            P("exp", "ctx", None),
            P("exp", "ctx", None),
            P("exp", None, None),
            P("exp", None, None),
        ),
        out_specs=(
            P("exp", "ctx", None),
            P("exp", "ctx", None),
            P("exp", "ctx", None),
            P("exp", "ctx", None),
            P("exp", "ctx", None),
        ),
        check_vma=False,
    )
```

```python
import jax
import jax.numpy as jnp
from jax import lax
from jax.experimental import pallas as pl
from jax.experimental.pallas import tpu as pltpu
from jax.sharding import PartitionSpec as P

HEAD_DIM = 128
EXP_DEV = 1


def rounded(x):
    return lax.optimization_barrier(x.astype(jnp.bfloat16)).astype(jnp.float32)


def general(
    queries, key_states, value_states, attended, output_grad, expert_ids, gate_weights, w_in, w_out
):
    tok = queries.shape[1]
    width = queries.shape[2]
    heads = width // HEAD_DIM
    nexp = lax.axis_size("exp")
    nctx = lax.axis_size("ctx")
    experts = EXP_DEV * nexp
    capacity = 3 * tok // experts
    attn_rows = attended[0]
    grad_rows = output_grad[0]
    route = expert_ids[0].reshape(-1)
    gates = gate_weights[0].reshape(-1)
    onehot = (route[:, None] == jnp.arange(experts, dtype=jnp.int32)[None, :]).astype(jnp.int32)
    slots = jnp.sum((jnp.cumsum(onehot, axis=0) - 1) * onehot, axis=1)
    target = route * capacity + slots
    placed = target[None, :] == jnp.arange(experts * capacity, dtype=jnp.int32)[:, None]
    picker = (
        placed.reshape(experts * capacity, tok, 2)
        .astype(jnp.float32)
        .sum(axis=2)
        .astype(jnp.bfloat16)
    )
    slot_gate = jnp.sum(jnp.where(placed, gates[None, :], 0.0), axis=1)
    sent_rows = jnp.dot(picker, attn_rows, preferred_element_type=jnp.float32).astype(jnp.bfloat16)
    sent_grads = (
        jnp.dot(picker, grad_rows, preferred_element_type=jnp.float32) * slot_gate[:, None]
    ).astype(jnp.bfloat16)
    shape = (nexp, EXP_DEV * capacity, width)
    got_rows, got_grads = (
        lax.all_to_all(sent_rows.reshape(shape), "exp", split_axis=0, concat_axis=0, tiled=True),
        lax.all_to_all(sent_grads.reshape(shape), "exp", split_axis=0, concat_axis=0, tiled=True),
    )

    def by_expert(values):
        return (
            values.reshape(nexp, EXP_DEV, capacity, -1)
            .transpose(1, 0, 2, 3)
            .reshape(EXP_DEV, nexp * capacity, -1)
        )

    rows_in = by_expert(got_rows)
    grads_in = by_expert(got_grads)
    upper = jnp.einsum("erd,edf->erf", rows_in, w_in, preferred_element_type=jnp.float32)
    sig = jax.nn.sigmoid(upper)
    act = (upper * sig).astype(jnp.bfloat16)
    act_grad = jnp.einsum("erd,efd->erf", grads_in, w_out, preferred_element_type=jnp.float32)
    up_grad = (act_grad * sig * (1.0 + upper * (1.0 - sig))).astype(jnp.bfloat16)
    row_back = jnp.einsum("erf,edf->erd", up_grad, w_in, preferred_element_type=jnp.float32).astype(
        jnp.bfloat16
    )
    first_term = jnp.einsum("erd,erf->edf", rows_in, up_grad, preferred_element_type=jnp.float32)
    second_term = jnp.einsum("erf,erd->efd", act, grads_in, preferred_element_type=jnp.float32)
    back_send = (
        row_back.reshape(EXP_DEV, nexp, capacity, width).transpose(1, 0, 2, 3).reshape(shape)
    )
    returned = lax.all_to_all(back_send, "exp", split_axis=0, concat_axis=0, tiled=True)
    back_sum = jnp.dot(
        picker.T, returned.reshape(experts * capacity, width), preferred_element_type=jnp.float32
    )
    attn_grad = (grad_rows.astype(jnp.float32) + back_sum).astype(jnp.bfloat16)
    first_sum, second_sum = (
        lax.psum_scatter(
            first_term.astype(jnp.bfloat16), "ctx", scatter_dimension=1, tiled=True
        ).astype(jnp.float32),
        lax.psum_scatter(
            second_term.astype(jnp.bfloat16), "ctx", scatter_dimension=1, tiled=True
        ).astype(jnp.float32),
    )
    w_in_grad = first_sum.astype(jnp.bfloat16)
    w_out_grad = second_sum.astype(jnp.bfloat16)
    scale = HEAD_DIM ** (-0.5)
    group = min(max(1, 512 // tok), nctx)
    blocks = nctx // group
    key_heads = key_states[0].reshape(tok, heads, HEAD_DIM)
    value_heads = value_states[0].reshape(tok, heads, HEAD_DIM)
    delta = jnp.sum(
        (attn_grad.astype(jnp.float32) * attn_rows.astype(jnp.float32)).reshape(
            tok, heads, HEAD_DIM
        ),
        axis=2,
    )
    query_all, grad_all = (
        lax.all_gather(queries[0], "ctx", axis=0, tiled=True),
        lax.all_gather(attn_grad, "ctx", axis=0, tiled=True),
    )
    span = group * tok
    query_blocks = query_all.reshape(blocks, span, heads, HEAD_DIM)
    grad_blocks = grad_all.reshape(blocks, span, heads, HEAD_DIM)

    def norm_part(carry, query_blk):
        scores = (
            jnp.einsum("qhd,khd->hqk", query_blk, key_heads, preferred_element_type=jnp.float32)
            * scale
        )
        return (carry, jnp.sum(jnp.exp(scores), axis=2).T)

    _, partial_sums = lax.scan(norm_part, jnp.zeros((), jnp.float32), query_blocks)
    own_delta = jnp.zeros((nctx * tok, heads), jnp.float32)
    own_delta = lax.dynamic_update_slice(own_delta, delta, (lax.axis_index("ctx") * tok, 0))
    totals, delta_all = (
        lax.psum(partial_sums.reshape(nctx * tok, heads).astype(jnp.bfloat16), "ctx").astype(
            jnp.float32
        ),
        lax.psum(own_delta.astype(jnp.bfloat16), "ctx").astype(jnp.float32),
    )
    norm_blocks = jnp.log(totals).reshape(blocks, span, heads)
    delta_blocks = delta_all.reshape(blocks, span, heads)

    def grad_step(carry, blk):
        key_acc, value_acc = carry
        query_blk, grad_blk, norm_blk, delta_blk = blk
        scores = (
            jnp.einsum("qhd,khd->hqk", query_blk, key_heads, preferred_element_type=jnp.float32)
            * scale
        )
        probs = jnp.exp(scores - norm_blk.T[:, :, None])
        probs_b = probs.astype(jnp.bfloat16)
        prob_grad = jnp.einsum(
            "qhd,khd->hqk", grad_blk, value_heads, preferred_element_type=jnp.float32
        )
        score_grad = (probs * (prob_grad - delta_blk.T[:, :, None])).astype(jnp.bfloat16)
        query_term = (
            jnp.einsum("hqk,khd->qhd", score_grad, key_heads, preferred_element_type=jnp.float32)
            * scale
        )
        split_grad = score_grad.reshape(heads, group, tok, tok)
        split_probs = probs_b.reshape(heads, group, tok, tok)
        split_query = query_blk.reshape(group, tok, heads, HEAD_DIM)
        split_out = grad_blk.reshape(group, tok, heads, HEAD_DIM)
        key_part = (
            jnp.einsum(
                "hgqk,gqhd->gkhd", split_grad, split_query, preferred_element_type=jnp.float32
            )
            * scale
        )
        value_part = jnp.einsum(
            "hgqk,gqhd->gkhd", split_probs, split_out, preferred_element_type=jnp.float32
        )
        key_acc = key_acc + jnp.sum(rounded(key_part), axis=0)
        value_acc = value_acc + jnp.sum(rounded(value_part), axis=0)
        return ((key_acc, value_acc), query_term)

    zero = jnp.zeros((tok, heads, HEAD_DIM), jnp.float32)
    (key_acc, value_acc), query_terms = lax.scan(
        grad_step, (zero, zero), (query_blocks, grad_blocks, norm_blocks, delta_blocks)
    )
    query_sum = lax.psum_scatter(
        query_terms.reshape(nctx * tok, width).astype(jnp.bfloat16),
        "ctx",
        scatter_dimension=0,
        tiled=True,
    )
    key_grad = key_acc.reshape(tok, width).astype(jnp.bfloat16)
    value_grad = value_acc.reshape(tok, width).astype(jnp.bfloat16)
    return (query_sum[None], key_grad[None], value_grad[None], w_in_grad, w_out_grad)


F32, BF16 = jnp.float32, jnp.bfloat16
NT = (((1,), (1,)), ((), ()))
TN = (((0,), (0,)), ((), ()))
WIDE = 512
EXPERTS = 8
SOON, LATER = (2, 3, 6), (0, 1, 7, 4, 5)
FIRST, LAST = (0, 1, 2, 3, 6), (7, 4, 5)


GROUPS = ((0, 2), (2, 3))


def grant(mebibytes):
    return pltpu.CompilerParams(vmem_limit_bytes=mebibytes << 20)


def vmem_specs(count):
    return [pl.BlockSpec(memory_space=pltpu.VMEM)] * count


def fill_payloads(partners, pick_ref, gate_ref, rows_ref, grads_ref, out_refs, capacity):
    spans = [slice(p * capacity, (p + 1) * capacity) for p in partners]
    pick = jnp.concatenate([pick_ref[span, :] for span in spans], axis=0)
    gate = jnp.concatenate([gate_ref[span, :] for span in spans], axis=0)
    for n in range(0, rows_ref.shape[1], WIDE):
        cols = slice(n, n + WIDE)
        rows = jnp.dot(pick, rows_ref[:, cols], preferred_element_type=F32).astype(BF16)
        grads = jnp.dot(pick, grads_ref[:, cols], preferred_element_type=F32) * gate
        grads = grads.astype(BF16)
        place = 0
        for b, p in enumerate(partners):
            span = slice(b * capacity, (b + 1) * capacity)
            if p in LAST:
                out_refs[place][:, cols] = rows[span]
                out_refs[place + 1][:, cols] = grads[span]
                place += 2
            else:
                out_refs[place][:capacity, cols] = rows[span]
                out_refs[place][capacity:, cols] = grads[span]
                place += 1


def payload_shapes(partners, capacity, width):
    one = jax.ShapeDtypeStruct((2 * capacity, width), BF16)
    part = jax.ShapeDtypeStruct((capacity, width), BF16)
    return tuple(x for p in partners for x in ((part, part) if p in LAST else (one,)))


def pick_slots(ids, gates, rows, grads, capacity):
    tok, width = rows.shape
    payloads = payload_shapes(SOON, capacity, width)
    given = (ids, gates, rows, grads)

    def kernel(*refs):
        pick_ref, gate_ref = refs[4:6]
        out_refs = refs[6 : 6 + len(payloads)]
        ids_ref, gates_ref, rows_ref, grads_ref = held = refs[-8:-4]
        copies = [pltpu.make_async_copy(a, b, s) for a, b, s in zip(refs[:4], held, refs[-4:])]
        for copy in copies:
            copy.start()
        copies[0].wait()
        copies[1].wait()
        me = lax.axis_index("exp")
        first, second = ids_ref[0:1, :] ^ me, ids_ref[1:2, :] ^ me
        expert = lax.broadcasted_iota(jnp.int32, (EXPERTS, tok), 0)
        is_first, is_second = first == expert, second == expert
        member = jnp.where(is_first | is_second, 1.0, 0.0)
        earlier = jnp.where(
            lax.broadcasted_iota(jnp.int32, (tok, tok), 0)
            < lax.broadcasted_iota(jnp.int32, (tok, tok), 1),
            1.0,
            0.0,
        )
        before = jnp.dot(member.astype(BF16), earlier.astype(BF16), preferred_element_type=F32)
        slot = jnp.where(member > 0, before, -1.0).astype(jnp.int32)
        gate = jnp.where(is_first, gates_ref[0:1, :], 0.0) + jnp.where(
            is_second, gates_ref[1:2, :], 0.0
        )
        place = lax.broadcasted_iota(jnp.int32, (capacity, tok), 0)
        for e in range(EXPERTS):
            chosen = jnp.where(slot[e : e + 1, :] == place, 1.0, 0.0)
            span = slice(e * capacity, (e + 1) * capacity)
            pick_ref[span, :] = chosen.astype(BF16)
            gate_ref[span, :] = jnp.sum(chosen * gate[e : e + 1, :], axis=1, keepdims=True)
        copies[2].wait()
        copies[3].wait()
        fill_payloads(SOON, pick_ref, gate_ref, rows_ref, grads_ref, out_refs, capacity)

    return pl.pallas_call(
        kernel,
        out_shape=(
            jax.ShapeDtypeStruct((EXPERTS * capacity, tok), BF16),
            jax.ShapeDtypeStruct((EXPERTS * capacity, 1), F32),
        )
        + payloads,
        in_specs=[pl.BlockSpec(memory_space=pltpu.HBM)] * 4,
        out_specs=tuple(vmem_specs(2 + len(payloads))),
        scratch_shapes=[pltpu.VMEM(x.shape, x.dtype) for x in given]
        + [pltpu.SemaphoreType.DMA] * 4,
        compiler_params=grant(20),
        name="pick_slots",
    )(*given)


def pick_rest(pick, gate, rows, grads, capacity):
    payloads = payload_shapes(LATER, capacity, rows.shape[1])

    def kernel(pick_ref, gate_ref, rows_ref, grads_ref, *out_refs):
        fill_payloads(LATER, pick_ref, gate_ref, rows_ref, grads_ref, out_refs, capacity)

    return pl.pallas_call(
        kernel,
        out_shape=payloads,
        in_specs=vmem_specs(4),
        out_specs=tuple(vmem_specs(len(payloads))),
        compiler_params=grant(20),
        name="pick_rest",
    )(pick, gate, rows, grads)


def upper_only(rows, w_first):
    capacity, width = rows[0].shape
    slots, hidden = len(rows) * capacity, w_first.shape[1]
    tile = 256

    def kernel(*refs):
        first_ref, upper_ref, act_ref = refs[len(rows) :]
        held = jnp.concatenate([r[...] for r in refs[: len(rows)]], axis=0)
        upper = jnp.dot(held, first_ref[...], preferred_element_type=F32)
        upper_ref[...] = upper
        act_ref[...] = (upper * jax.nn.sigmoid(upper)).astype(BF16)

    return pl.pallas_call(
        kernel,
        grid=(hidden // tile,),
        out_shape=(
            jax.ShapeDtypeStruct((slots, hidden), F32),
            jax.ShapeDtypeStruct((slots, hidden), BF16),
        ),
        in_specs=[pl.BlockSpec((capacity, width), lambda f: (0, 0))] * len(rows)
        + [pl.BlockSpec((width, tile), lambda f: (0, f))],
        out_specs=(pl.BlockSpec((slots, tile), lambda f: (0, f)),) * 2,
        compiler_params=grant(20),
        name="upper_only",
    )(*rows, w_first)


def run_experts(rows, grads, upper, w_first, w_second):
    count, (width, hidden) = len(grads), w_first.shape
    capacity = grads[0][0].shape[0] - grads[0][1]
    slots = count * capacity
    tile = 256
    arrays = [a for a, _ in grads]
    extra = [] if upper is None else [upper]

    def kernel(*refs):
        ins = refs[:count]
        first_ref, second_ref = refs[count : count + 2]
        outs = refs[count + 2 + len(extra) :]
        total_ref = outs[-1]
        cotangents = jnp.concatenate(
            [r[low : low + capacity, :] for r, (_, low) in zip(ins, grads)], axis=0
        )
        if extra:
            upper, (up_ref, *back_refs) = refs[count + 2][...], outs[:-1]
        else:
            act_ref, up_ref, *back_refs = outs[:-1]
            held = jnp.concatenate(
                [r[low : low + capacity, :] for r, (_, low) in zip(ins, rows)], axis=0
            )
            upper = jnp.dot(held, first_ref[...], preferred_element_type=F32)
        act_grad = lax.dot_general(cotangents, second_ref[...], NT, preferred_element_type=F32)
        sig = jax.nn.sigmoid(upper)
        if not extra:
            act_ref[...] = (upper * sig).astype(BF16)
        up = (act_grad * sig * (1.0 + upper * (1.0 - sig))).astype(BF16)
        up_ref[...] = up
        back = lax.dot_general(up, first_ref[...], NT, preferred_element_type=F32)
        step, last = pl.program_id(0), hidden // tile - 1

        @pl.when(step == 0)
        def _():
            total_ref[...] = back

        @pl.when((step > 0) & (step < last))
        def _():
            total_ref[...] += back

        @pl.when(step == last)
        def _():
            total = (total_ref[...] + back).astype(BF16)
            for b, ref in enumerate(back_refs):
                ref[...] = total[b * capacity : (b + 1) * capacity]

    narrow = pl.BlockSpec((slots, tile), lambda f: (0, f))
    hidden_outs = 1 if extra else 2
    outs = pl.pallas_call(
        kernel,
        grid=(hidden // tile,),
        out_shape=(jax.ShapeDtypeStruct((slots, hidden), BF16),) * hidden_outs
        + (jax.ShapeDtypeStruct((capacity, width), BF16),) * count,
        in_specs=[pl.BlockSpec(a.shape, lambda f: (0, 0)) for a in arrays]
        + [
            pl.BlockSpec((width, tile), lambda f: (0, f)),
            pl.BlockSpec((tile, width), lambda f: (f, 0)),
        ]
        + [narrow] * len(extra),
        out_specs=(narrow,) * hidden_outs
        + (pl.BlockSpec((capacity, width), lambda f: (0, 0)),) * count,
        scratch_shapes=[pltpu.VMEM((slots, width), F32)],
        compiler_params=grant(20),
        name="run_experts",
    )(*arrays, w_first, w_second, *extra)
    return (*outs[:hidden_outs], outs[hidden_outs:])


def weight_terms(left, right, capacity, places, pieces):
    rows, cols = left[0][0].shape[1], right[0][0].shape[1]
    share = rows // 4
    size = share // pieces
    outs = len(places) * pieces
    count = len(left)

    def gather(refs, parts):
        return jnp.concatenate(
            [
                r[...] if low is None else r[low : low + capacity, :]
                for r, (_, low) in zip(refs, parts)
            ],
            axis=0,
        )

    def kernel(*refs):
        turned_ref = refs[-1]
        turned_ref[...] = gather(refs[:count], left).T
        held = gather(refs[count:], right)
        out_refs = refs[count + len(right) : -1]
        me = lax.axis_index("ctx")
        for n in range(outs):
            begin = (me ^ places[n // pieces]) * share + n % pieces * size
            rows_here = pl.ds(pl.multiple_of(begin, size), size)
            out_refs[n][...] = jnp.dot(
                turned_ref[rows_here, :], held, preferred_element_type=F32
            ).astype(BF16)

    slots = sum(a.shape[0] if low is None else capacity for a, low in left)
    return pl.pallas_call(
        kernel,
        out_shape=(jax.ShapeDtypeStruct((size, cols), BF16),) * outs,
        in_specs=vmem_specs(count + len(right)),
        out_specs=tuple(vmem_specs(outs)),
        scratch_shapes=[pltpu.VMEM((rows, slots), BF16)],
        compiler_params=grant(20),
        name="weight_terms",
    )(*[a for a, _ in left], *[a for a, _ in right])


def add_back(pick, returned, grads, column, size):
    tok = grads.shape[0]
    capacity = returned[0].shape[0]

    def kernel(pick_ref, grads_ref, *refs):
        back = jnp.concatenate([r[...] for r in refs[:-1]], axis=0)
        total = lax.dot_general(pick_ref[...], back, TN, preferred_element_type=F32)
        refs[-1][...] = (grads_ref[...].astype(F32) + total).astype(BF16)

    return pl.pallas_call(
        kernel,
        grid=(1,),
        out_shape=jax.ShapeDtypeStruct((tok, size), BF16),
        in_specs=[pl.BlockSpec(pick.shape, lambda i: (0, 0))]
        + [pl.BlockSpec((tok, size), lambda i: (0, column // size))]
        + [pl.BlockSpec((capacity, size), lambda i: (0, column // size))] * len(returned),
        out_specs=pl.BlockSpec((tok, size), lambda i: (0, 0)),
        compiler_params=grant(20),
        name="add_back",
    )(pick, grads, *returned)


def head_specs(count, tok, step, first=0):
    return [pl.BlockSpec((tok, step * HEAD_DIM), lambda h: (0, h + first // step))] * count


def stacked(refs, cols):
    return jnp.concatenate([r[:, cols] for r in refs], axis=0)


def with_delta(grads, attended):
    product = grads.astype(F32) * attended.astype(F32)
    return jnp.concatenate([grads, product.astype(BF16)], axis=1)


def with_ones(values):
    return jnp.concatenate([values, jnp.full_like(values, -1.0)], axis=1)


def probabilities(query_blocks, key_blocks):
    tok, width = query_blocks[0].shape
    heads, count = width // HEAD_DIM, len(query_blocks)
    total = count * tok
    scale = HEAD_DIM**-0.5
    step = 2

    def kernel(*refs):
        by_query_ref, by_key_ref = refs[2 * count :]
        for h in range(step):
            cols = slice(h * HEAD_DIM, (h + 1) * HEAD_DIM)
            q, k = stacked(refs[:count], cols), stacked(refs[count : 2 * count], cols)
            row = jnp.exp(lax.dot_general(q[:tok], k, NT, preferred_element_type=F32) * scale)
            by_query_ref[h] = (row / jnp.sum(row, axis=1, keepdims=True)).astype(BF16)
            col = jnp.exp(lax.dot_general(k[:tok], q, NT, preferred_element_type=F32) * scale)
            norm = jnp.sum(col, axis=0, keepdims=True)
            for b in range(1, count):
                other = lax.dot_general(
                    k[b * tok : (b + 1) * tok], q, NT, preferred_element_type=F32
                )
                norm = norm + jnp.sum(jnp.exp(other * scale), axis=0, keepdims=True)
            by_key_ref[h] = (col / norm).astype(BF16)

    shape = jax.ShapeDtypeStruct((heads, tok, total), BF16)
    return pl.pallas_call(
        kernel,
        grid=(heads // step,),
        out_shape=(shape, shape),
        in_specs=head_specs(2 * count, tok, step),
        out_specs=(pl.BlockSpec((step, tok, total), lambda h: (h, 0, 0)),) * 2,
        compiler_params=grant(20),
        name="probabilities",
    )(*query_blocks, *key_blocks)


def query_side(span, g, attended, probs, key_blocks, value_blocks, before):
    first, last = span
    tok, width = attended.shape
    count, step = len(key_blocks), 4
    scale = HEAD_DIM**-0.5
    carried = [] if before is None else [before]

    def kernel(*refs):
        g_ref, att_ref, probs_ref = refs[:3]
        out_ref = refs[-1]
        for h in range(step):
            cols = slice(h * HEAD_DIM, (h + 1) * HEAD_DIM)
            keys = stacked(refs[3 : 3 + count], cols)
            values = with_ones(stacked(refs[3 + count : 3 + 2 * count], cols))
            both = with_delta(g_ref[:, cols], att_ref[:, cols])
            diff = lax.dot_general(both, values, NT, preferred_element_type=F32)
            score = (probs_ref[h].astype(F32) * diff).astype(BF16)
            grad = jnp.dot(score, keys, preferred_element_type=F32) * scale
            out_ref[:, cols] = grad.astype(BF16)

    return pl.pallas_call(
        kernel,
        grid=((last - first) // step,),
        out_shape=jax.ShapeDtypeStruct((tok, width), BF16),
        in_specs=head_specs(1, tok, step)
        + head_specs(1, tok, step, first)
        + [pl.BlockSpec((step, tok, count * tok), lambda h: (h + first // step, 0, 0))]
        + head_specs(2 * count, tok, step, first)
        + [pl.BlockSpec(memory_space=pl.ANY)] * len(carried),
        out_specs=head_specs(1, tok, step, first)[0],
        input_output_aliases={3 + 2 * count: 0} if carried else {},
        compiler_params=grant(20),
        name="query_side",
    )(g, attended, probs, *key_blocks, *value_blocks, *carried)


def key_side(span, g_blocks, attended_blocks, probs, query_blocks, values, before):
    first, last = span
    tok, width = values.shape
    count, step = len(g_blocks), 4
    scale = HEAD_DIM**-0.5
    carried = [] if before is None else list(before)

    def kernel(*refs):
        probs_ref, v_ref = refs[:2]
        key_ref, value_ref = refs[-2:]
        for h in range(step):
            cols = slice(h * HEAD_DIM, (h + 1) * HEAD_DIM)
            g = stacked(refs[2 : 2 + count], cols)
            both = with_delta(g, stacked(refs[2 + count : 2 + 2 * count], cols))
            queries = stacked(refs[2 + 2 * count : 2 + 3 * count], cols)
            diff = lax.dot_general(
                with_ones(v_ref[:, cols]), both, NT, preferred_element_type=F32
            )
            probs = probs_ref[h]
            score = (probs.astype(F32) * diff).astype(BF16)
            grad = jnp.dot(score, queries, preferred_element_type=F32) * scale
            key_ref[:, cols] = grad.astype(BF16)
            value_ref[:, cols] = jnp.dot(probs, g, preferred_element_type=F32).astype(BF16)

    shape = jax.ShapeDtypeStruct((tok, width), BF16)
    return pl.pallas_call(
        kernel,
        grid=((last - first) // step,),
        out_shape=(shape, shape),
        in_specs=[pl.BlockSpec((step, tok, count * tok), lambda h: (h + first // step, 0, 0))]
        + head_specs(1, tok, step, first)
        + head_specs(count, tok, step)
        + head_specs(2 * count, tok, step, first)
        + [pl.BlockSpec(memory_space=pl.ANY)] * len(carried),
        out_specs=tuple(head_specs(2, tok, step, first)),
        input_output_aliases={2 + 3 * count: 0, 3 + 3 * count: 1} if carried else {},
        compiler_params=grant(20),
        name="key_side",
    )(probs, values, *g_blocks, *attended_blocks, *query_blocks, *carried)


def swap(values, axis, bits):
    return lax.ppermute(values, axis, [(i, i ^ bits) for i in range(lax.axis_size(axis))])


def stream_blocks(own):
    across = swap(own, "ctx", 2)
    return own, swap(own, "ctx", 1), across, swap(across, "ctx", 1)


def across_chips(across, opposite):
    opposite = swap(opposite, "ctx", 1)
    sent = (across.astype(F32) + opposite.astype(F32)).astype(BF16)
    return swap(sent, "ctx", 2)


def total_rows(own, beside, others):
    beside = swap(beside, "ctx", 1)
    other = jnp.concatenate(others, axis=0).astype(F32)
    return (own.astype(F32) + beside.astype(F32) + other).astype(BF16)[None]


def trade(values, partner):
    return swap(values, "exp", partner) if partner else values


def quick(
    queries, key_states, value_states, attended, output_grad, expert_ids, gate_weights, w_in, w_out
):
    tok, width = queries.shape[1:]
    heads = width // HEAD_DIM
    capacity = 3 * tok // EXPERTS
    ids, gates = expert_ids[0].T, gate_weights[0].T
    attn_rows, grad_rows = attended[0], output_grad[0]
    inputs = (attn_rows, grad_rows, capacity)

    pick, slot_gate, *soon = pick_slots(ids, gates, *inputs)
    later = pick_rest(pick, slot_gate, *inputs)
    sent = iter((*soon, *later))
    rows, grads = {}, {}
    for p in SOON + LATER:
        if p in LAST:
            rows[p] = (trade(next(sent), p), 0)
            grads[p] = (trade(next(sent), p), 0)
        else:
            payload = trade(next(sent), p)
            rows[p], grads[p] = (payload, 0), (payload, capacity)

    query_blocks = stream_blocks(queries[0])
    key_blocks = stream_blocks(key_states[0])
    value_blocks = stream_blocks(value_states[0])
    attended_blocks = stream_blocks(attn_rows)
    by_query, by_key = probabilities(query_blocks, key_blocks)

    weights = (w_in[0], w_out[0])
    soon_rows, soon_grads = [rows[p] for p in FIRST], [grads[p] for p in FIRST]
    late_rows, late_grads = [rows[p] for p in LAST], [grads[p] for p in LAST]
    act_a, up_a, first = run_experts(soon_rows, soon_grads, None, *weights)
    upper_b, act_b = upper_only([a for a, _ in late_rows], w_in[0])
    up_b, last = run_experts([], late_grads, upper_b, *weights)
    back = {p: trade(rows, p) for p, rows in zip(FIRST + LAST, (*first, *last))}
    back = [back[p] for p in range(EXPERTS)]

    out_terms = ([(act_a, None), (act_b, None)], soon_grads + late_grads, capacity)
    in_terms = (soon_rows + late_rows, [(up_a, None), (up_b, None)], capacity)
    out_3, out_2 = weight_terms(*out_terms, (3, 2), 1)
    low_3, high_3, low_2, high_2 = weight_terms(*in_terms, (3, 2), 2)
    out_1, out_0 = weight_terms(*out_terms, (1, 0), 1)
    in_1, in_0 = weight_terms(*in_terms, (1, 0), 1)
    out_other = across_chips(out_2, out_3)
    low_other = across_chips(low_2, low_3)
    high_other = across_chips(high_2, high_3)
    w_out_grad = total_rows(out_0, out_1, [out_other])
    w_in_grad = total_rows(in_0, in_1, [low_other, high_other])

    query_grad = pair = None
    for low, high in GROUPS:
        span = (low * heads // 3, high * heads // 3)
        column, size = low * width // 3, (high - low) * width // 3
        g = add_back(pick, back, grad_rows, column, size)
        g_blocks = stream_blocks(g)
        query_grad = query_side(span, g, attn_rows, by_query, key_blocks, value_blocks, query_grad)
        pair = key_side(
            span, g_blocks, attended_blocks, by_key, query_blocks,
            value_states[0], pair,
        )
    key_grad, value_grad = pair
    return (query_grad[None], key_grad[None], value_grad[None], w_in_grad, w_out_grad)


def per_device(queries, *rest):
    tok, width = queries.shape[1:]
    fits = lax.axis_size("ctx") == 4 and lax.axis_size("exp") == EXPERTS
    fits = fits and tok % 128 == 0 and (3 * tok // EXPERTS) % 16 == 0
    if fits and width % (12 * HEAD_DIM) == 0 and rest[-1].shape[1] % 256 == 0:
        return quick(queries, *rest)
    return general(queries, *rest)


def solution(mesh):
    return jax.shard_map(
        per_device,
        mesh=mesh,
        in_specs=(
            P("exp", "ctx", None),
            P("exp", "ctx", None),
            P("exp", "ctx", None),
            P("exp", "ctx", None),
            P("exp", "ctx", None),
            P("exp", "ctx", None),
            P("exp", "ctx", None),
            P("exp", None, None),
            P("exp", None, None),
        ),
        out_specs=(
            P("exp", "ctx", None),
            P("exp", "ctx", None),
            P("exp", "ctx", None),
            P("exp", "ctx", None),
            P("exp", "ctx", None),
        ),
        check_vma=False,
    )
```
